256 devices in a mesh: leaf: 32 (over x_hi, z, core), head: 8 (over x_lo, y).
Axes of the slice: x: 4 (x_hi: 2, x_lo: 2; x = x_hi * 2 + x_lo), y: 4, z: 8, core: 2. Of those that a mesh axis runs over, the one named last changes fastest.
Arguments:
- latents: bfloat16 [2048, 512], P('leaf'), may hold values from -14 to 14
- queries: bfloat16 [4096, 64, 128], P('leaf', 'head'), may hold values from -14 to 14
- grad_out: bfloat16 [4096, 64, 128], P('leaf', 'head'), may hold values from -6 to 6
- key_up_matrix: bfloat16 [64, 128, 512], P('head'), may hold values from -0.25 to 0.25
- value_up_matrix: bfloat16 [64, 512, 128], P('head'), may hold values from -0.25 to 0.25
- parents: int32 [256], replicated, may hold values from 0 to 254, as said below
- branch_node: int32 [32, 8], P('leaf'), may hold values from 0 to 255
- branch_lengths: int32 [32, 8], P('leaf'), may hold values from 1 to 40, 128 in all within a row
Outputs:
- d_queries: bfloat16 [4096, 64, 128], P('leaf', 'head')
- d_latents: float32 [2048, 512], P('leaf')
The draws below stay inside these ranges and needn't reach their ends.
Inputs may be any that keep to these rules, and one draw needn't show every extreme that they name: parents[0] = 0 and parents[n] < n for every n >= 1.
All inputs are finite; a program needn't handle non-finite values.
Results may differ from the reference program's by a relative error of at most 0.025.
The reference program's roundings to bfloat16 on the way count: a program that leaves them out, or rounds other values in their place, can miss the bound.
Values may be sent and summed in bfloat16 or wider, within the bound.
A program may use at most 64 MiB of HBM per device.

```python
import math
import jax
import jax.numpy as jnp
import numpy as np
from jax import lax

KEY_VALUE_RANK = 512
HEAD_COUNT = 64
QUERY_KEY_PLAIN = 128
VALUE_WIDTH = 128
Q_DEV = 128
BR_DEV = 8
NODE_LEN = 8
BR_MOST = 40
PROMPT_ROWS = 2048
NODES = 256
TOKENS = 4096
BLOCKS = 32


def draw_parents(key, part):
    places = jnp.arange(NODES, dtype=jnp.int32)
    back = jax.random.randint(key, (NODES,), 0, 4, dtype=jnp.int32)
    back = jnp.where(places == NODES - 1, 0, back).astype(jnp.int32)
    return jnp.maximum(places - 1 - back, 0).astype(jnp.int32)


def draw_latents(key, part):
    value_rows = jnp.clip(jax.random.normal(jax.random.fold_in(key, 13), (PROMPT_ROWS, KEY_VALUE_RANK), jnp.float32), -6.0, 6.0)
    return value_rows.astype(jnp.bfloat16)


def draw_queries(key, part):
    value_rows = jnp.clip(jax.random.normal(jax.random.fold_in(key, 23), (TOKENS, HEAD_COUNT, QUERY_KEY_PLAIN), jnp.float32), -6.0, 6.0)
    return value_rows.astype(jnp.bfloat16)


def set_ends(values, stream_key, least, largest):
    spot = [jax.random.randint(jax.random.fold_in(stream_key, axis), (), 0, length) for axis, length in enumerate(values.shape)]
    widest = values.shape.index(max(values.shape))
    beside = spot[:widest] + [(spot[widest] + 1) % values.shape[widest]] + spot[widest + 1:]
    return values.at[tuple(spot)].set(least).at[tuple(beside)].set(largest)


def levels(stream_key, dims, shards, smallest, top_value):
    loudness = 1.0
    for position, parts in shards:
        steps = jax.random.uniform(jax.random.fold_in(jax.random.fold_in(stream_key, 6), position), (parts,), jnp.float32, smallest / len(shards), top_value / len(shards))
        loudness = loudness * jnp.repeat(jnp.exp(steps), dims[position] // parts).reshape((-1,) + (1,) * (len(dims) - 1 - position))
    return loudness


def profile(number_of, total, most, lean):
    portions = [(1 << 20) // math.isqrt(standing ** lean) + 1 for standing in range(2, number_of + 1)]
    surplus, holding = total - most - (number_of - 1), [1] * (number_of - 1)
    while surplus > 0:
        movable = [i for i in range(number_of - 1) if holding[i] < most]
        whole, budget = sum([portions[i] for i in movable]), surplus
        for i in movable:
            extra = min(most - holding[i], max(1, budget * portions[i] // whole), surplus)
            holding[i] = holding[i] + extra
            surplus = surplus - extra
    return np.array([most] + holding)


def ragged(stream_key, number_of, total, limit, lean):
    if number_of == 2:
        one = jax.random.randint(stream_key, (), max(1, total - limit), min(limit, total - 1) + 1)
        return jnp.stack([one, total - one])
    tallies = jnp.asarray(profile(number_of, total, limit, lean), jnp.int32)
    pairs = (number_of - 1) // 2
    giver, receiver = tallies[1:1 + 2 * pairs:2], tallies[2:2 + 2 * pairs:2]
    margin = jnp.minimum(giver - 1, limit - receiver)
    moved = jax.random.randint(jax.random.fold_in(stream_key, 1), (pairs,), 0, 1 << 20) % (margin + 1)
    tallies = tallies.at[1:1 + 2 * pairs:2].set(giver - moved).at[2:2 + 2 * pairs:2].set(receiver + moved)
    return tallies[jax.random.permutation(jax.random.fold_in(stream_key, 2), number_of)]


def bell_draw(own_key, dims, spread, reach, cuts=(), kind=jnp.bfloat16):
    level = levels(own_key, dims, cuts, -0.22, 0.18) if cuts else 1.0
    values = jax.random.normal(own_key, dims, jnp.float32) * spread * level
    return jnp.minimum(jnp.maximum(values, -reach), reach).astype(kind)


def setup_inputs(seed: int = 0) -> dict:
    streams_of = jax.random.split(jax.random.key(seed), 9)
    return {
        "latents": draw_latents(jax.random.fold_in(streams_of[8], 71), 0),
        "queries": draw_queries(jax.random.fold_in(streams_of[8], 71), 0),
        "grad_out": bell_draw(streams_of[2], (TOKENS, HEAD_COUNT, VALUE_WIDTH), 1.0, 6.0, ((0, 32), (1, 8))),
        "key_up_matrix": bell_draw(streams_of[3], (HEAD_COUNT, QUERY_KEY_PLAIN, KEY_VALUE_RANK), KEY_VALUE_RANK ** -0.5, 0.25, ((0, 8),)),
        "value_up_matrix": bell_draw(streams_of[4], (HEAD_COUNT, KEY_VALUE_RANK, VALUE_WIDTH), KEY_VALUE_RANK ** -0.5, 0.25, ((0, 8),)),
        "parents": draw_parents(jax.random.fold_in(streams_of[8], 71), 0),
        "branch_node": set_ends(jax.random.randint(streams_of[6], (BLOCKS, BR_DEV), 0, NODES), jax.random.fold_in(streams_of[6], 1), 0, NODES - 1).astype(jnp.int32),
        "branch_lengths": jax.vmap(lambda own: ragged(own, BR_DEV, Q_DEV, BR_MOST, 2))(jax.random.split(streams_of[7], BLOCKS)).reshape((BLOCKS, BR_DEV)).astype(jnp.int32),
    }


softmax_scale = 192.0 ** -0.5
masked_score = -1.0e30


def ancestry(parents):
    node_count = parents.shape[0]
    indices = jnp.arange(node_count, dtype=jnp.int32)
    linked = (parents[:, None] == indices[None, :]) | (indices[:, None] == indices[None, :])
    closure = linked.astype(jnp.float32)
    for squaring in range(node_count.bit_length()):
        closure = jnp.minimum(jnp.dot(closure, closure, precision=lax.Precision.HIGHEST), 1.0)
    return closure


def token_nodes(lengths_row, nodes_row, tok_count):
    bounds = jnp.cumsum(lengths_row).astype(jnp.int32)
    places = jnp.arange(tok_count, dtype=jnp.int32)
    branch_of = jnp.sum((places[:, None] >= bounds[None, :]).astype(jnp.int32), axis=1)
    select = branch_of[:, None] == jnp.arange(lengths_row.shape[0], dtype=jnp.int32)[None, :]
    return jnp.sum(jnp.where(select, nodes_row[None, :], 0), axis=1).astype(jnp.int32)


def live_keys(node_list, closure):
    node_count = closure.shape[0]
    select = (node_list[:, None] == jnp.arange(node_count, dtype=jnp.int32)[None, :]).astype(jnp.float32)
    reached = jnp.dot(select, closure, precision=lax.Precision.HIGHEST) > 0.5
    return jnp.repeat(reached, NODE_LEN, axis=1)


def rounded(value_rows):
    return lax.optimization_barrier(value_rows.astype(jnp.bfloat16)).astype(jnp.float32)


def reference(latents, queries, grad_out, key_up_matrix, value_up_matrix, parents, branch_node, branch_lengths):
    closure = ancestry(parents)
    node_lists = jax.vmap(token_nodes, in_axes=(0, 0, None))(branch_lengths, branch_node, Q_DEV)
    keys_wide = latents.astype(jnp.float32)
    key_up_wide = key_up_matrix.astype(jnp.float32)
    value_up_wide = value_up_matrix.astype(jnp.float32)
    query_blocks = queries.reshape(BLOCKS, Q_DEV, HEAD_COUNT, QUERY_KEY_PLAIN)
    grad_blocks = grad_out.reshape(BLOCKS, Q_DEV, HEAD_COUNT, VALUE_WIDTH)

    def one_block(latent_grad, inputs):
        query_block, grad_block, node_list = inputs
        usable = live_keys(node_list, closure)[:, None, :]
        query_latent = rounded(jnp.einsum('thd,hdc->thc', query_block.astype(jnp.float32), key_up_wide))
        grad_latent = rounded(jnp.einsum('thv,hcv->thc', grad_block.astype(jnp.float32), value_up_wide))
        logits = jnp.where(usable, softmax_scale * jnp.einsum('thc,kc->thk', query_latent, keys_wide), masked_score)
        running_max = jnp.max(logits, axis=-1)
        weights = jnp.where(usable, jnp.exp(logits - running_max[..., None]), 0.0)
        denom = jnp.sum(weights, axis=-1)
        attended = jnp.einsum('thk,kc->thc', rounded(weights), keys_wide) / denom[..., None]
        log_norm = running_max + jnp.log(denom)
        delta = jnp.sum(grad_latent * attended, axis=-1)
        probs = jnp.where(usable, jnp.exp(logits - log_norm[..., None]), 0.0)
        grad_weights = jnp.einsum('thc,kc->thk', grad_latent, keys_wide)
        grad_scores = rounded(probs * (grad_weights - delta[..., None]))
        query_grad = rounded(softmax_scale * jnp.einsum('thk,kc->thc', grad_scores, keys_wide))
        d_query = jnp.einsum('thc,hdc->thd', query_grad, key_up_wide).astype(jnp.bfloat16)
        contrib = softmax_scale * jnp.einsum('thk,thc->kc', grad_scores, query_latent)
        contrib = contrib + jnp.einsum('thk,thc->kc', rounded(probs), grad_latent)
        return latent_grad + contrib, d_query

    initial_gradient = jnp.zeros((PROMPT_ROWS, KEY_VALUE_RANK), jnp.float32)
    latent_grad, d_queries = lax.scan(one_block, initial_gradient, (query_blocks, grad_blocks, node_lists))
    return d_queries.reshape(TOKENS, HEAD_COUNT, QUERY_KEY_PLAIN), latent_grad
```

```python
import jax
import jax.numpy as jnp
from jax import lax
from jax.experimental import pallas as pl
from jax.experimental.pallas import tpu as pltpu
from jax.sharding import PartitionSpec as P

MESH = pl.DeviceIdType.MESH
NODE_LEN = 8
SCALE = 192.0 ** (-0.5)
LOG2E = 1.4426950408889634
MASKED = -1e30
LAG = 3
F32 = jnp.float32
BF16 = jnp.bfloat16


def dot(a, b):
    return jnp.dot(a, b, preferred_element_type=F32)


def place():
    leaf = lax.axis_index("leaf")
    head = lax.axis_index("head")
    x = (leaf // 16) * 2 + head // 4
    return x, lax.rem(head, 4), lax.rem(leaf // 2, 8), lax.rem(leaf, 2)


def device(x, y, z, c):
    return ((x // 2) * 16 + z * 2 + c, lax.rem(x, 2) * 4 + y)


def step_offset(s):
    half = (s + 1) // 2
    return 4 + jnp.where(lax.rem(s, 2) == 1, -half, half)


def kernel(
    lat_ref, par_ref, node_ref, len_ref, q_hbm, g_hbm, ku_hbm, vu_hbm,
    dq_ref, dl_ref,
    q_in, g_in, ku, vu, wide, keys, keys_t, ql, gl, ql_t, gl_t, live_t,
    w_buf, gw_buf, gs_buf, m_grp, m_run, l_run, d_run,
    cont, core_out, core_in, axis_out, axis_in, z_out, z_in, z_own,
    sum_a, sum_b, last_a, last_b, out_a, out_b,
    in_sem, ag_send, x_recv, z_recv, c_recv,
    core_send, core_recv, ax_send, ax_recv, zs_send, zs_recv,
    t1_send, t1_recv, t2_send, t2_recv,
):
    x, y, z, c = place()
    x_hi = x // 2
    at = lambda dx, dy, dz: device(
        lax.rem(x + dx + 4, 4), lax.rem(y + dy + 4, 4), lax.rem(z + dz + 8, 8), c
    )
    sibling = device(x, y, z, 1 - c)
    partner = device(3 - x, y, z, c)

    loads = [
        pltpu.make_async_copy(src, dst, in_sem.at[i])
        for i, (src, dst) in enumerate(((q_hbm, q_in), (ku_hbm, ku), (g_hbm, g_in), (vu_hbm, vu)))
    ]
    for load in loads:
        load.start()

    barrier = pltpu.get_barrier_semaphore()
    peers = [sibling, at(0, 0, 1), at(0, 0, -1)]
    peers += [at(k, 0, 0) for k in (1, 2, 3)] + [at(0, k, 0) for k in (1, 2, 3)]
    for peer in peers:
        pl.semaphore_signal(barrier, inc=1, device_id=peer, device_id_type=MESH)
    keys[z, c, x_hi] = lat_ref[...]
    pl.semaphore_wait(barrier, len(peers))

    sent = []

    def send(block, recv_sem, peer):
        copy = pltpu.make_async_remote_copy(
            src_ref=block, dst_ref=block, send_sem=ag_send.at[len(sent)], recv_sem=recv_sem,
            device_id=peer, device_id_type=MESH,
        )
        copy.start()
        sent.append(copy)

    def arrived(block, recv_sem):
        pltpu.make_async_remote_copy(
            src_ref=block, dst_ref=block, send_sem=ag_send.at[0], recv_sem=recv_sem,
            device_id=sibling, device_id_type=MESH,
        ).wait_recv()

    mine = (x_hi, 1 - x_hi)
    own = keys.at[z, c, x_hi]
    send(own, x_recv.at[0], partner)
    send(own, z_recv.at[0, 0, 0], at(0, 0, 1))
    send(own, z_recv.at[1, 0, 0], at(0, 0, -1))
    send(own, c_recv.at[0, 0], sibling)

    def latents_of(src_ref, mat, out_ref, out_t_ref, turned):
        wide[...] = src_ref[...].astype(F32).reshape(wide.shape)
        for h in range(8):
            rows = wide[pl.ds(h, 128, stride=8), :].astype(BF16)
            if turned:
                val = lax.dot_general(
                    rows, mat[h], (((1,), (1,)), ((), ())), preferred_element_type=F32
                )
            else:
                val = dot(rows, mat[h])
            low = val.astype(BF16)
            out_ref[h * 128 : (h + 1) * 128, :] = low
            out_t_ref[:, h * 128 : (h + 1) * 128] = low.T

    loads[0].wait()
    loads[1].wait()
    latents_of(q_in, ku, ql, ql_t, False)

    other = keys.at[z, c, 1 - x_hi]
    arrived(other, x_recv.at[0])
    send(other, z_recv.at[0, 0, 1], at(0, 0, 1))
    send(other, z_recv.at[1, 0, 1], at(0, 0, -1))
    send(other, c_recv.at[0, 1], sibling)

    loads[2].wait()
    loads[3].wait()
    latents_of(g_in, vu, gl, gl_t, True)

    def forward(dist):
        for way in (0, 1):
            for kind in (0, 1):
                if dist == 4 and way != kind:
                    continue
                sign = 1 if way == 0 else -1
                origin = lax.rem(z - sign * dist + 8, 8)
                block = keys.at[origin, c, mine[kind]]
                arrived(block, z_recv.at[way, dist - 1, kind])
                if dist < 3 or (dist == 3 and way == kind):
                    send(block, z_recv.at[way, dist, kind], at(0, 0, sign))
                slot = 2 * dist - 1 + (way if dist < 4 else 0)
                send(block, c_recv.at[slot, kind], sibling)

    forward(1)

    above = lax.broadcasted_iota(jnp.int32, (256, 256), 0)
    below = lax.broadcasted_iota(jnp.int32, (256, 256), 1)
    linked = (above == par_ref[...]) | (above == below)
    reach = jnp.where(linked, 1.0, 0.0).astype(BF16)
    for _ in range(8):
        reach = jnp.minimum(dot(reach, reach), 1.0).astype(BF16)
    spot = lax.broadcasted_iota(jnp.int32, (256, 128), 1)
    node = lax.broadcasted_iota(jnp.int32, (256, 128), 0)
    token_node = jnp.full((256, 128), node_ref[0, 0], jnp.int32)
    bound = len_ref[0, 0]
    for b in range(1, 8):
        token_node = jnp.where(spot >= bound, node_ref[0, b], token_node)
        bound = bound + len_ref[0, b]
    picked = jnp.where(token_node == node, 1.0, 0.0).astype(BF16)
    live_t[...] = dot(reach, picked).astype(BF16)

    m_run[...] = jnp.full(m_run.shape, MASKED, F32)
    l_run[...] = jnp.zeros(l_run.shape, F32)
    d_run[...] = jnp.zeros(d_run.shape, F32)

    def score_group(plane):
        group = keys[plane].reshape(256, 512)
        keys_t[:, pl.ds(pl.multiple_of(plane * 256, 256), 256)] = group.T
        row = lax.broadcasted_iota(jnp.int32, (256, 256), 0)
        col = lax.broadcasted_iota(jnp.int32, (256, 256), 1)
        half, which, inner = row // 128, lax.rem(row // 64, 2), lax.rem(row, 64) // NODE_LEN
        key_node = ((which * 8 + plane) * 2 + half) * NODE_LEN + inner
        spread = jnp.where(key_node == col, 1.0, 0.0).astype(BF16)
        bias = (dot(spread, live_t[...]) - 1.0) * (-MASKED)
        bias = jnp.concatenate([bias, bias], axis=1)
        for tile in range(4):
            cols = slice(tile * 256, (tile + 1) * 256)
            s = dot(group, ql_t[:, cols]) * (SCALE * LOG2E) + bias
            gw = dot(group, gl_t[:, cols])
            m_old = m_run[:, cols]
            m_new = jnp.maximum(m_old, jnp.max(s, axis=0, keepdims=True))
            w = jnp.exp2(s - m_new)
            alpha = jnp.exp2(m_old - m_new)
            l_run[:, cols] = alpha * l_run[:, cols] + jnp.sum(w, axis=0, keepdims=True)
            low = w.astype(BF16).astype(F32)
            d_run[:, cols] = alpha * d_run[:, cols] + jnp.sum(low * gw, axis=0, keepdims=True)
            m_run[:, cols] = m_new
            m_grp[plane, :, cols] = m_new
            w_buf[plane, :, cols] = w
            gw_buf[plane, :, cols] = gw

    def sibling_blocks(origin, slot):
        for kind in (0, 1):
            arrived(keys.at[origin, 1 - c, mine[kind]], c_recv.at[slot, kind])

    def scores(slots):
        first, count = slots

        def body(i, _):
            slot = first + i
            dist = (slot + 1) // 2
            sign = jnp.where(lax.rem(slot, 2) == 1, -1, 1)
            score_group(lax.rem(z + sign * dist + 8, 8))
            return 0

        lax.fori_loop(0, count, body, 0)

    sibling_blocks(z, 0)
    scores((0, 1))
    for dist in (1, 2, 3):
        forward(dist + 1)
        sibling_blocks(lax.rem(z - dist + 8, 8), 2 * dist - 1)
        sibling_blocks(lax.rem(z + dist, 8), 2 * dist)
        scores((2 * dist - 1, 2))
    sibling_blocks(lax.rem(z + 4, 8), 7)
    scores((7, 1))

    inv = 1.0 / l_run[...]
    l_run[...] = inv
    d_run[...] = d_run[...] * inv

    def core_copy(s):
        return pltpu.make_async_remote_copy(
            src_ref=core_out.at[s], dst_ref=core_in.at[s], send_sem=core_send.at[s],
            recv_sem=core_recv.at[s], device_id=sibling, device_id_type=MESH,
        )

    def axis_copies(s):
        copies = []
        for part in (0, 1):
            for k in (1, 2, 3):
                place_of = lax.rem((x if part == 0 else y) + k, 4)
                copies.append(
                    pltpu.make_async_remote_copy(
                        src_ref=axis_out.at[s, part, place_of], dst_ref=axis_in.at[s, part, k - 1],
                        send_sem=ax_send.at[s, part, k - 1], recv_sem=ax_recv.at[s, part, k - 1],
                        device_id=at(k, 0, 0) if part == 0 else at(0, k, 0), device_id_type=MESH,
                    )
                )
        return copies

    def z_copy(s):
        return pltpu.make_async_remote_copy(
            src_ref=z_out.at[s], dst_ref=z_in.at[s], send_sem=zs_send.at[s],
            recv_sem=zs_recv.at[s], device_id=at(0, 0, step_offset(s)), device_id_type=MESH,
        )

    def contribution(s):
        plane = lax.rem(z + step_offset(s), 8)
        total = None
        for tile in range(4):
            cols = slice(tile * 256, (tile + 1) * 256)
            factor = jnp.exp2(m_grp[plane, :, cols] - m_run[:, cols]) * l_run[:, cols]
            p = w_buf[plane, :, cols] * factor
            gs = (p * (gw_buf[plane, :, cols] - d_run[:, cols])).astype(BF16)
            gs_buf[pl.ds(pl.multiple_of(plane * 256, 256), 256), cols] = gs
            term = dot(gs, ql[cols, :]) * SCALE + dot(p.astype(BF16), gl[cols, :])
            total = term if total is None else total + term
        slot = lax.rem(s, 2)
        cont[slot] = total.reshape(2, 2, 64, 512)
        for part in (0, 1):
            for j in range(4):
                core_out[s, part, j] = cont[
                    slot, 1 - c, :, part * 32 : (part + 1) * 32, j * 128 : (j + 1) * 128
                ].astype(BF16)
        core_copy(s).start()

    def core_sum(s):
        core_copy(s).wait()
        slot = lax.rem(s, 2)
        for part in (0, 1):
            for j in range(4):
                axis_out[s, part, j] = (
                    cont[slot, c, :, part * 32 : (part + 1) * 32, j * 128 : (j + 1) * 128]
                    + core_in[s, part, j].astype(F32)
                ).astype(BF16)
        for copy in axis_copies(s):
            copy.start()

    def axis_sum(s, last):
        for copy in axis_copies(s):
            copy.wait()
        for part in (0, 1):
            total = axis_out[s, part, x if part == 0 else y].astype(F32)
            for k in range(3):
                total = total + axis_in[s, part, k].astype(F32)
            if last:
                z_own[part] = total
            else:
                z_out[s, part] = total.astype(BF16)
        if not last:
            z_copy(s).start()

    def reduce_step(s, _):
        contribution(s)

        @pl.when(s >= 1)
        def _():
            core_sum(s - 1)

        @pl.when(s >= 1 + LAG)
        def _():
            axis_sum(s - 1 - LAG, False)

        return 0

    lax.fori_loop(0, 8, reduce_step, 0)

    def query_tile(tile):
        cols = slice(tile * 256, (tile + 1) * 256)
        grad = (dot(keys_t[...], gs_buf[:, cols]) * SCALE).astype(BF16)
        for i in (0, 1):
            h = 2 * tile + i
            out = dot(ku[h], grad[:, i * 128 : (i + 1) * 128])
            wide[pl.ds(h, 128, stride=8), :] = out.T

    core_sum(7)
    query_tile(0)
    for s in range(7 - LAG, 7):
        axis_sum(s, False)
    query_tile(1)
    axis_sum(7, True)
    for s in range(7):
        z_copy(s).wait()
    for part in (0, 1):
        total = z_own[part]
        for s in range(7):
            total = total + z_in[s, part].astype(F32)
        if part == 0:
            sum_a[y] = total.astype(BF16)
        else:
            out_b[...] = total.astype(BF16)
            sum_b[x] = out_b[x_hi]

    first = []
    for k in (1, 2, 3):
        first.append(
            pltpu.make_async_remote_copy(
                src_ref=sum_a.at[y], dst_ref=sum_a.at[y], send_sem=t1_send.at[0, k - 1],
                recv_sem=t1_recv.at[0, k - 1], device_id=at(0, k, 0), device_id_type=MESH,
            )
        )
        their_hi = lax.rem(x + k, 4) // 2
        first.append(
            pltpu.make_async_remote_copy(
                src_ref=out_b.at[their_hi], dst_ref=sum_b.at[x], send_sem=t1_send.at[1, k - 1],
                recv_sem=t1_recv.at[1, k - 1], device_id=at(k, 0, 0), device_id_type=MESH,
            )
        )
    for copy in first:
        copy.start()
    query_tile(2)
    query_tile(3)
    dq_ref[...] = wide[...].reshape(128, 8, 128).astype(BF16)
    for copy in first:
        copy.wait()

    out_a[...] = (
        sum_a[0].astype(F32) + sum_a[1].astype(F32) + sum_a[2].astype(F32) + sum_a[3].astype(F32)
    ).astype(BF16)
    last_a[x] = out_a[x_hi]
    last_b[y] = (
        sum_b[0].astype(F32) + sum_b[1].astype(F32) + sum_b[2].astype(F32) + sum_b[3].astype(F32)
    ).astype(BF16)
    second = []
    for k in (1, 2, 3):
        their_hi = lax.rem(x + k, 4) // 2
        second.append(
            pltpu.make_async_remote_copy(
                src_ref=out_a.at[their_hi], dst_ref=last_a.at[x], send_sem=t2_send.at[0, k - 1],
                recv_sem=t2_recv.at[0, k - 1], device_id=at(k, 0, 0), device_id_type=MESH,
            )
        )
        second.append(
            pltpu.make_async_remote_copy(
                src_ref=last_b.at[y], dst_ref=last_b.at[y], send_sem=t2_send.at[1, k - 1],
                recv_sem=t2_recv.at[1, k - 1], device_id=at(0, k, 0), device_id_type=MESH,
            )
        )
    for copy in second:
        copy.start()
    for copy in sent:
        copy.wait_send()
    for copy in second:
        copy.wait()
    for j in range(4):
        dl_ref[0:32, j * 128 : (j + 1) * 128] = last_a[j].astype(F32)
        dl_ref[32:64, j * 128 : (j + 1) * 128] = last_b[j].astype(F32)


def on_device(
    latents, queries, grad_out, key_up_matrix, value_up_matrix, parents, branch_node, branch_lengths
):
    vmem = pl.BlockSpec(memory_space=pltpu.VMEM)
    smem = pl.BlockSpec(memory_space=pltpu.SMEM)
    anywhere = pl.BlockSpec(memory_space=pl.ANY)
    dma = pltpu.SemaphoreType.DMA
    tile = (2, 32, 128)
    return pl.pallas_call(
        kernel,
        name="tree_attention_backward",
        out_shape=(
            jax.ShapeDtypeStruct((128, 8, 128), BF16),
            jax.ShapeDtypeStruct((64, 512), F32),
        ),
        in_specs=[vmem, vmem, smem, smem, anywhere, anywhere, anywhere, anywhere],
        out_specs=(vmem, vmem),
        scratch_shapes=[
            pltpu.VMEM((128, 8, 128), BF16),
            pltpu.VMEM((128, 8, 128), BF16),
            pltpu.VMEM((8, 128, 512), BF16),
            pltpu.VMEM((8, 512, 128), BF16),
            pltpu.VMEM((1024, 128), F32),
            pltpu.VMEM((8, 2, 2, 64, 512), BF16),
            pltpu.VMEM((512, 2048), BF16),
            pltpu.VMEM((1024, 512), BF16),
            pltpu.VMEM((1024, 512), BF16),
            pltpu.VMEM((512, 1024), BF16),
            pltpu.VMEM((512, 1024), BF16),
            pltpu.VMEM((256, 128), BF16),
            pltpu.VMEM((8, 256, 1024), F32),
            pltpu.VMEM((8, 256, 1024), F32),
            pltpu.VMEM((2048, 1024), BF16),
            pltpu.VMEM((8, 1, 1024), F32),
            pltpu.VMEM((1, 1024), F32),
            pltpu.VMEM((1, 1024), F32),
            pltpu.VMEM((1, 1024), F32),
            pltpu.VMEM((2, 2, 2, 64, 512), F32),
            pltpu.VMEM((8, 2, 4) + tile, BF16),
            pltpu.VMEM((8, 2, 4) + tile, BF16),
            pltpu.VMEM((8, 2, 4) + tile, BF16),
            pltpu.VMEM((8, 2, 3) + tile, BF16),
            pltpu.VMEM((7, 2) + tile, BF16),
            pltpu.VMEM((7, 2) + tile, BF16),
            pltpu.VMEM((2,) + tile, F32),
            pltpu.VMEM((4,) + tile, BF16),
            pltpu.VMEM((4, 32, 128), BF16),
            pltpu.VMEM((4, 32, 128), BF16),
            pltpu.VMEM((4, 32, 128), BF16),
            pltpu.VMEM(tile, BF16),
            pltpu.VMEM(tile, BF16),
            dma((4,)),
            dma((35,)),
            dma((1,)),
            dma((2, 4, 2)),
            dma((8, 2)),
            dma((8,)),
            dma((8,)),
            dma((8, 2, 3)),
            dma((8, 2, 3)),
            dma((7,)),
            dma((7,)),
            dma((2, 3)),
            dma((2, 3)),
            dma((2, 3)),
            dma((2, 3)),
        ],
        compiler_params=pltpu.CompilerParams(
            collective_id=0, has_side_effects=True, vmem_limit_bytes=58 * 1024 * 1024
        ),
    )(
        latents, parents.reshape(1, 256), branch_node, branch_lengths,
        queries, grad_out, key_up_matrix, value_up_matrix,
    )


def solution(mesh):
    placed = (
        P("leaf", None),
        P("leaf", "head", None),
        P("leaf", "head", None),
        P("head", None, None),
        P("head", None, None),
        P(),
        P("leaf", None),
        P("leaf", None),
    )
    return jax.shard_map(
        on_device,
        mesh=mesh,
        in_specs=placed,
        out_specs=(P("leaf", "head", None), P("leaf", None)),
        check_vma=False,
    )
```

```python
import jax
import jax.numpy as jnp
from jax import lax
from jax.experimental import pallas as pl
from jax.experimental.pallas import tpu as pltpu
from jax.sharding import PartitionSpec as P

MESH = pl.DeviceIdType.MESH
NODE_LEN = 8
SCALE = 192.0 ** (-0.5)
LOG2E = 1.4426950408889634
MASKED = -1e30
F32 = jnp.float32
BF16 = jnp.bfloat16


def dot(a, b):
    return jnp.dot(a, b, preferred_element_type=F32)


def place():
    leaf = lax.axis_index("leaf")
    head = lax.axis_index("head")
    x = (leaf // 16) * 2 + head // 4
    return x, lax.rem(head, 4), lax.rem(leaf // 2, 8), lax.rem(leaf, 2)


def device(x, y, z, c):
    return ((x // 2) * 16 + z * 2 + c, lax.rem(x, 2) * 4 + y)


def step_offset(s):
    return (4, 3, 5, 2, 6, 1, 7, 0)[s]


def kernel(
    lat_ref, par_ref, node_ref, len_ref, q_hbm, g_hbm, ku_hbm, vu_hbm,
    dq_ref, dl_ref,
    q_in, g_in, ku, vu, wide, keys, keys_t, ql, gl, ql_t, gl_t, live_t,
    w_buf, gw_buf, gs_buf, m_grp, m_run, l_run, d_run,
    cont, core_out, core_in, axis_out, axis_in, z_out, z_in, z_own,
    sum_a, sum_b, last_a, last_b, out_a, out_b,
    in_sem, ag_send, x_recv, z_recv, n_recv, c_recv,
    core_send, core_recv, ax_send, ax_recv, zs_send, zs_recv,
    t1_send, t1_recv, t2_send, t2_recv,
):
    x, y, z, c = place()
    x_hi = x // 2
    at = lambda dx, dy, dz: device(
        lax.rem(x + dx + 4, 4), lax.rem(y + dy + 4, 4), lax.rem(z + dz + 8, 8), c
    )
    sibling = device(x, y, z, 1 - c)
    partner = device(3 - x, y, z, c)

    loads = [
        pltpu.make_async_copy(src, dst, in_sem.at[i])
        for i, (src, dst) in enumerate(((q_hbm, q_in), (ku_hbm, ku), (g_hbm, g_in), (vu_hbm, vu)))
    ]
    for load in loads:
        load.start()

    barrier = pltpu.get_barrier_semaphore()
    peers = [sibling] + [at(0, 0, k) for k in range(1, 8)]
    peers += [at(k, 0, 0) for k in (1, 2, 3)] + [at(0, k, 0) for k in (1, 2, 3)]
    for peer in peers:
        pl.semaphore_signal(barrier, inc=1, device_id=peer, device_id_type=MESH)
    keys[z, c, x_hi] = lat_ref[...].reshape(4, 16, 512)
    pl.semaphore_wait(barrier, len(peers))

    sent = []

    def send(block, recv_sem, peer):
        copy = pltpu.make_async_remote_copy(
            src_ref=block, dst_ref=block, send_sem=ag_send.at[len(sent)], recv_sem=recv_sem,
            device_id=peer, device_id_type=MESH,
        )
        copy.start()
        sent.append(copy)

    def arrived(block, recv_sem):
        pltpu.make_async_remote_copy(
            src_ref=block, dst_ref=block, send_sem=ag_send.at[0], recv_sem=recv_sem,
            device_id=sibling, device_id_type=MESH,
        ).wait_recv()

    colour = lambda x, y: lax.rem(y + 2 * lax.rem(x, 2), 4)
    flip = device(x + 1 - 2 * lax.rem(x, 2), y, z, c)
    neighbours = (at(0, 1, 0), at(0, -1, 0), flip)
    mine = colour(x, y)
    theirs = (lax.rem(mine + 3, 4), lax.rem(mine + 1, 4), lax.rem(mine + 2, 4))
    kinds = (x_hi, 1 - x_hi)
    far_first = (4, 3, 5, 2, 6, 1, 7)
    near_first = (1, 7, 2, 6, 3, 5, 4)

    def spread_z(kind):
        for k in far_first:
            send(keys.at[z, c, kinds[kind], mine], z_recv.at[k - 1, kind], at(0, 0, k))

    send(keys.at[z, c, x_hi], x_recv.at[0], partner)
    spread_z(0)
    send(keys.at[z, c, x_hi], c_recv.at[7, 0], sibling)

    def latents_of(src_ref, mat, out_ref, out_t_ref, turned):
        wide[...] = src_ref[...].astype(F32).reshape(wide.shape)
        for h in range(8):
            rows = wide[pl.ds(h, 128, stride=8), :].astype(BF16)
            if turned:
                val = lax.dot_general(
                    rows, mat[h], (((1,), (1,)), ((), ())), preferred_element_type=F32
                )
            else:
                val = dot(rows, mat[h])
            low = val.astype(BF16)
            out_ref[h * 128 : (h + 1) * 128, :] = low
            out_t_ref[:, h * 128 : (h + 1) * 128] = low.T

    loads[0].wait()
    loads[1].wait()
    latents_of(q_in, ku, ql, ql_t, False)

    arrived(keys.at[z, c, 1 - x_hi], x_recv.at[0])
    spread_z(1)
    send(keys.at[z, c, 1 - x_hi], c_recv.at[7, 1], sibling)

    loads[2].wait()
    loads[3].wait()
    latents_of(g_in, vu, gl, gl_t, True)

    def spread_replicas(kind):
        for k in near_first:
            piece = keys.at[lax.rem(z - k + 8, 8), c, kinds[kind], mine]
            arrived(piece, z_recv.at[k - 1, kind])
            for i in range(3):
                send(piece, n_recv.at[k - 1, kind, i], neighbours[i])

    above = lax.broadcasted_iota(jnp.int32, (256, 256), 0)
    below = lax.broadcasted_iota(jnp.int32, (256, 256), 1)
    linked = (above == par_ref[...]) | (above == below)
    reach = jnp.where(linked, 1.0, 0.0).astype(BF16)
    for _ in range(8):
        reach = jnp.minimum(dot(reach, reach), 1.0).astype(BF16)
    spot = lax.broadcasted_iota(jnp.int32, (256, 128), 1)
    node = lax.broadcasted_iota(jnp.int32, (256, 128), 0)
    token_node = jnp.full((256, 128), node_ref[0, 0], jnp.int32)
    bound = len_ref[0, 0]
    for b in range(1, 8):
        token_node = jnp.where(spot >= bound, node_ref[0, b], token_node)
        bound = bound + len_ref[0, b]
    picked = jnp.where(token_node == node, 1.0, 0.0).astype(BF16)
    live_t[...] = dot(reach, picked).astype(BF16)

    m_run[...] = jnp.full(m_run.shape, MASKED, F32)
    l_run[...] = jnp.zeros(l_run.shape, F32)
    d_run[...] = jnp.zeros(d_run.shape, F32)

    spread_replicas(0)

    def score_blocks(kind, planes):
        which = kinds[kind]
        rows = 128 * len(planes)
        row = lax.broadcasted_iota(jnp.int32, (rows, 256), 0)
        col = lax.broadcasted_iota(jnp.int32, (rows, 256), 1)
        plane_of = jnp.zeros((rows, 256), jnp.int32)
        for n, plane in enumerate(planes):
            plane_of = jnp.where(row // 128 == n, plane, plane_of)
        half, inner = lax.rem(row // 64, 2), lax.rem(row, 64) // NODE_LEN
        key_node = ((which * 8 + plane_of) * 2 + half) * NODE_LEN + inner
        spread = jnp.where(key_node == col, 1.0, 0.0).astype(BF16)
        bias = (dot(spread, live_t[...]) - 1.0) * (-MASKED)
        bias = jnp.concatenate([bias, bias], axis=1)
        group = jnp.concatenate([keys[plane, :, which].reshape(128, 512) for plane in planes], axis=0)
        for tile in range(4):
            cols = slice(tile * 256, (tile + 1) * 256)
            s = dot(group, ql_t[:, cols]) * (SCALE * LOG2E) + bias
            gw = dot(group, gl_t[:, cols])
            m_old = m_run[:, cols]
            m_new = jnp.maximum(m_old, jnp.max(s, axis=0, keepdims=True))
            w = jnp.exp2(s - m_new)
            alpha = jnp.exp2(m_old - m_new)
            l_run[:, cols] = alpha * l_run[:, cols] + jnp.sum(w, axis=0, keepdims=True)
            low = w.astype(BF16).astype(F32)
            d_run[:, cols] = alpha * d_run[:, cols] + jnp.sum(low * gw, axis=0, keepdims=True)
            m_run[:, cols] = m_new
            for n, plane in enumerate(planes):
                part = slice(n * 128, (n + 1) * 128)
                m_grp[plane, which, :, cols] = m_new
                w_buf[plane, :, which, :, cols] = w[part].reshape(2, 64, 256)
                gw_buf[plane, :, which, :, cols] = gw[part].reshape(2, 64, 256)

    def complete(kind, steps):
        for k in steps:
            block = keys.at[lax.rem(z - k + 8, 8), c, kinds[kind]]
            for i in range(3):
                piece = keys.at[lax.rem(z - k + 8, 8), c, kinds[kind], theirs[i]]
                arrived(piece, n_recv.at[k - 1, kind, i])
            send(block, c_recv.at[k - 1, kind], sibling)

    def score_from(kind, steps):
        planes = []
        for k in steps:
            plane = lax.rem(z - k + 8, 8)
            arrived(keys.at[plane, 1 - c, kinds[kind]], c_recv.at[(k - 1) % 8, kind])
            if kind == 1:
                keys_t[:, pl.ds(pl.multiple_of(plane * 256, 256), 256)] = (
                    keys[plane].reshape(256, 512).T
                )
            planes.append(plane)
        score_blocks(kind, planes)

    spread_replicas(1)
    complete(0, near_first)
    score_from(0, (0,) + near_first[:3])
    complete(1, near_first[:3])
    score_from(0, near_first[3:])
    complete(1, near_first[3:])
    score_from(1, (0,) + near_first[:3])
    score_from(1, near_first[3:])

    inv = 1.0 / l_run[...]
    l_run[...] = inv
    d_run[...] = d_run[...] * inv

    def core_copy(s):
        return pltpu.make_async_remote_copy(
            src_ref=core_out.at[s], dst_ref=core_in.at[s], send_sem=core_send.at[s],
            recv_sem=core_recv.at[s], device_id=sibling, device_id_type=MESH,
        )

    def axis_copies(s):
        copies = []
        for part in (0, 1):
            for k in (1, 2, 3):
                place_of = lax.rem((x if part == 0 else y) + k, 4)
                copies.append(
                    pltpu.make_async_remote_copy(
                        src_ref=axis_out.at[s, part, place_of], dst_ref=axis_in.at[s, part, k - 1],
                        send_sem=ax_send.at[s, part, k - 1], recv_sem=ax_recv.at[s, part, k - 1],
                        device_id=at(k, 0, 0) if part == 0 else at(0, k, 0), device_id_type=MESH,
                    )
                )
        return copies

    def z_copy(s):
        return pltpu.make_async_remote_copy(
            src_ref=z_out.at[s], dst_ref=z_in.at[s], send_sem=zs_send.at[s],
            recv_sem=zs_recv.at[s], device_id=at(0, 0, step_offset(s)), device_id_type=MESH,
        )

    def contribution(*steps):
        planes = [lax.rem(z + step_offset(s), 8) for s in steps]
        total = None
        for tile in range(4):
            cols = slice(tile * 256, (tile + 1) * 256)
            probs, grads = [], []
            for plane in planes:
                factor = [
                    jnp.exp2(m_grp[plane, which, :, cols] - m_run[:, cols]) * l_run[:, cols]
                    for which in (0, 1)
                ]
                for half in (0, 1):
                    for which in (0, 1):
                        p = w_buf[plane, half, which, :, cols] * factor[which]
                        gw = gw_buf[plane, half, which, :, cols]
                        grads.append((p * (gw - d_run[:, cols])).astype(BF16))
                        probs.append(p.astype(BF16))
                gs_buf[pl.ds(pl.multiple_of(plane * 256, 256), 256), cols] = jnp.concatenate(
                    grads[-4:], axis=0
                )
            gs, p_low = jnp.concatenate(grads, axis=0), jnp.concatenate(probs, axis=0)
            term = dot(gs, ql[cols, :]) * SCALE + dot(p_low, gl[cols, :])
            total = term if total is None else total + term
        for n, s in enumerate(steps):
            slot = s % 4
            cont[slot] = total[n * 256 : (n + 1) * 256].reshape(2, 2, 64, 512)
            for part in (0, 1):
                for j in range(4):
                    core_out[s, part, j] = cont[
                        slot, 1 - c, :, part * 32 : (part + 1) * 32, j * 128 : (j + 1) * 128
                    ].astype(BF16)
            core_copy(s).start()

    def core_sum(s):
        core_copy(s).wait()
        slot = s % 4
        for part in (0, 1):
            for j in range(4):
                axis_out[s, part, j] = (
                    cont[slot, c, :, part * 32 : (part + 1) * 32, j * 128 : (j + 1) * 128]
                    + core_in[s, part, j].astype(F32)
                ).astype(BF16)
        for copy in axis_copies(s):
            copy.start()

    def axis_sum(s, last):
        for copy in axis_copies(s):
            copy.wait()
        for part in (0, 1):
            total = axis_out[s, part, x if part == 0 else y].astype(F32)
            for k in range(3):
                total = total + axis_in[s, part, k].astype(F32)
            if last:
                z_own[part] = total
            else:
                z_out[s, part] = total.astype(BF16)
        if not last:
            z_copy(s).start()

    def query_tile(tile):
        cols = slice(tile * 512, (tile + 1) * 512)
        grad = (dot(keys_t[...], gs_buf[:, cols]) * SCALE).astype(BF16)
        for i in range(4):
            h = 4 * tile + i
            out = dot(ku[h], grad[:, i * 128 : (i + 1) * 128])
            wide[pl.ds(h, 128, stride=8), :] = out.T

    contribution(0)
    contribution(1, 2)
    core_sum(0)
    contribution(3, 4)
    core_sum(1)
    core_sum(2)
    axis_sum(0, False)
    contribution(5, 6)
    core_sum(3)
    core_sum(4)
    contribution(7)
    core_sum(5)
    core_sum(6)
    axis_sum(1, False)
    axis_sum(2, False)
    core_sum(7)
    axis_sum(3, False)
    axis_sum(4, False)
    query_tile(0)
    axis_sum(5, False)
    axis_sum(6, False)
    axis_sum(7, True)
    for s in range(7):
        z_copy(s).wait()
    for part in (0, 1):
        total = z_own[part]
        for s in range(7):
            total = total + z_in[s, part].astype(F32)
        if part == 0:
            sum_a[y] = total.astype(BF16)
        else:
            out_b[...] = total.astype(BF16)
            sum_b[x] = out_b[x_hi]

    first = []
    for k in (1, 2, 3):
        first.append(
            pltpu.make_async_remote_copy(
                src_ref=sum_a.at[y], dst_ref=sum_a.at[y], send_sem=t1_send.at[0, k - 1],
                recv_sem=t1_recv.at[0, k - 1], device_id=at(0, k, 0), device_id_type=MESH,
            )
        )
        their_hi = lax.rem(x + k, 4) // 2
        first.append(
            pltpu.make_async_remote_copy(
                src_ref=out_b.at[their_hi], dst_ref=sum_b.at[x], send_sem=t1_send.at[1, k - 1],
                recv_sem=t1_recv.at[1, k - 1], device_id=at(k, 0, 0), device_id_type=MESH,
            )
        )
    for copy in first:
        copy.start()
    query_tile(1)
    dq_ref[...] = wide[...].reshape(128, 8, 128).astype(BF16)
    for copy in first:
        copy.wait()

    out_a[...] = (
        sum_a[0].astype(F32) + sum_a[1].astype(F32) + sum_a[2].astype(F32) + sum_a[3].astype(F32)
    ).astype(BF16)
    last_a[x] = out_a[x_hi]
    last_b[y] = (
        sum_b[0].astype(F32) + sum_b[1].astype(F32) + sum_b[2].astype(F32) + sum_b[3].astype(F32)
    ).astype(BF16)
    second = []
    for k in (1, 2, 3):
        their_hi = lax.rem(x + k, 4) // 2
        second.append(
            pltpu.make_async_remote_copy(
                src_ref=out_a.at[their_hi], dst_ref=last_a.at[x], send_sem=t2_send.at[0, k - 1],
                recv_sem=t2_recv.at[0, k - 1], device_id=at(k, 0, 0), device_id_type=MESH,
            )
        )
        second.append(
            pltpu.make_async_remote_copy(
                src_ref=last_b.at[y], dst_ref=last_b.at[y], send_sem=t2_send.at[1, k - 1],
                recv_sem=t2_recv.at[1, k - 1], device_id=at(0, k, 0), device_id_type=MESH,
            )
        )
    for copy in second:
        copy.start()
    for copy in sent:
        copy.wait_send()
    for copy in second:
        copy.wait()
    for j in range(4):
        dl_ref[0:32, j * 128 : (j + 1) * 128] = last_a[j].astype(F32)
        dl_ref[32:64, j * 128 : (j + 1) * 128] = last_b[j].astype(F32)


def hand_over(dq_in, dl_in, dq_out, dl_out):
    dq_out[...] = dq_in[...]
    dl_out[...] = dl_in[...]


def on_device(
    latents, queries, grad_out, key_up_matrix, value_up_matrix, parents, branch_node, branch_lengths
):
    vmem = pl.BlockSpec(memory_space=pltpu.VMEM)
    smem = pl.BlockSpec(memory_space=pltpu.SMEM)
    anywhere = pl.BlockSpec(memory_space=pl.ANY)
    dma = pltpu.SemaphoreType.DMA
    tile = (2, 32, 128)
    d_queries, d_latents = pl.pallas_call(
        kernel,
        name="tree_attention_backward",
        out_shape=(
            jax.ShapeDtypeStruct((128, 8, 128), BF16),
            jax.ShapeDtypeStruct((64, 512), F32),
        ),
        in_specs=[vmem, vmem, smem, smem, anywhere, anywhere, anywhere, anywhere],
        out_specs=(vmem, vmem),
        scratch_shapes=[
            pltpu.VMEM((128, 8, 128), BF16),
            pltpu.VMEM((128, 8, 128), BF16),
            pltpu.VMEM((8, 128, 512), BF16),
            pltpu.VMEM((8, 512, 128), BF16),
            pltpu.VMEM((1024, 128), F32),
            pltpu.VMEM((8, 2, 2, 4, 16, 512), BF16),
            pltpu.VMEM((512, 2048), BF16),
            pltpu.VMEM((1024, 512), BF16),
            pltpu.VMEM((1024, 512), BF16),
            pltpu.VMEM((512, 1024), BF16),
            pltpu.VMEM((512, 1024), BF16),
            pltpu.VMEM((256, 128), BF16),
            pltpu.VMEM((8, 2, 2, 64, 1024), F32),
            pltpu.VMEM((8, 2, 2, 64, 1024), F32),
            pltpu.VMEM((2048, 1024), BF16),
            pltpu.VMEM((8, 2, 1, 1024), F32),
            pltpu.VMEM((1, 1024), F32),
            pltpu.VMEM((1, 1024), F32),
            pltpu.VMEM((1, 1024), F32),
            pltpu.VMEM((4, 2, 2, 64, 512), F32),
            pltpu.VMEM((8, 2, 4) + tile, BF16),
            pltpu.VMEM((8, 2, 4) + tile, BF16),
            pltpu.VMEM((8, 2, 4) + tile, BF16),
            pltpu.VMEM((8, 2, 3) + tile, BF16),
            pltpu.VMEM((7, 2) + tile, BF16),
            pltpu.VMEM((7, 2) + tile, BF16),
            pltpu.VMEM((2,) + tile, F32),
            pltpu.VMEM((4,) + tile, BF16),
            pltpu.VMEM((4, 32, 128), BF16),
            pltpu.VMEM((4, 32, 128), BF16),
            pltpu.VMEM((4, 32, 128), BF16),
            pltpu.VMEM(tile, BF16),
            pltpu.VMEM(tile, BF16),
            dma((4,)),
            dma((73,)),
            dma((1,)),
            dma((7, 2)),
            dma((7, 2, 3)),
            dma((8, 2)),
            dma((8,)),
            dma((8,)),
            dma((8, 2, 3)),
            dma((8, 2, 3)),
            dma((7,)),
            dma((7,)),
            dma((2, 3)),
            dma((2, 3)),
            dma((2, 3)),
            dma((2, 3)),
        ],
        compiler_params=pltpu.CompilerParams(
            collective_id=0, has_side_effects=True, vmem_limit_bytes=58 * 1024 * 1024
        ),
    )(
        latents, parents.reshape(1, 256), branch_node, branch_lengths,
        queries, grad_out, key_up_matrix, value_up_matrix,
    )
    return pl.pallas_call(
        hand_over,
        name="hand_over",
        out_shape=(
            jax.ShapeDtypeStruct((128, 8, 128), BF16),
            jax.ShapeDtypeStruct((64, 512), F32),
        ),
        in_specs=[vmem, vmem],
        out_specs=(vmem, vmem),
    )(d_queries, d_latents)


def solution(mesh):
    placed = (
        P("leaf", None),
        P("leaf", "head", None),
        P("leaf", "head", None),
        P("head", None, None),
        P("head", None, None),
        P(),
        P("leaf", None),
        P("leaf", None),
    )
    return jax.shard_map(
        on_device,
        mesh=mesh,
        in_specs=placed,
        out_specs=(P("leaf", "head", None), P("leaf", None)),
        check_vma=False,
    )
```

```python
import jax
import jax.numpy as jnp
from jax import lax
from jax.experimental import pallas as pl
from jax.experimental.pallas import tpu as pltpu
from jax.sharding import PartitionSpec as P

MESH = pl.DeviceIdType.MESH
NODE_LEN = 8
SCALE = 192.0 ** (-0.5)
LOG2E = 1.4426950408889634
MASKED = -1e30
F32 = jnp.float32
BF16 = jnp.bfloat16


def dot(a, b):
    return jnp.dot(a, b, preferred_element_type=F32)


def place():
    leaf = lax.axis_index("leaf")
    head = lax.axis_index("head")
    x = (leaf // 16) * 2 + head // 4
    return x, lax.rem(head, 4), lax.rem(leaf // 2, 8), lax.rem(leaf, 2)


def device(x, y, z, c):
    return ((x // 2) * 16 + z * 2 + c, lax.rem(x, 2) * 4 + y)


def step_offset(s):
    return (4, 3, 5, 2, 6, 1, 7, 0)[s]


def kernel(
    lat_hbm, par_hbm, node_hbm, len_hbm, q_hbm, g_hbm, ku_hbm, vu_hbm,
    dq_ref, dl_ref,
    lat_ref, par_ref, node_ref, len_ref, q_in, g_in, ku, vu, wide, keys, keys_t, ql, gl, ql_t, gl_t, live_t,
    w_buf, gw_buf, gs_buf, m_grp, m_run, l_run, d_run,
    cont, core_out, core_in, axis_out, axis_in, z_out, z_in, z_own,
    sum_a, sum_b, last_a, last_b, out_a, out_b,
    in_sem, ag_send, x_recv, z_recv, n_recv, c_recv,
    core_send, core_recv, ax_send, ax_recv, zs_send, zs_recv,
    t1_send, t1_recv, t2_send, t2_recv,
):
    x, y, z, c = place()
    x_hi = x // 2
    at = lambda dx, dy, dz: device(
        lax.rem(x + dx + 4, 4), lax.rem(y + dy + 4, 4), lax.rem(z + dz + 8, 8), c
    )
    sibling = device(x, y, z, 1 - c)
    partner = device(3 - x, y, z, c)

    pairs = (
        (lat_hbm, lat_ref), (q_hbm, q_in), (ku_hbm, ku), (g_hbm, g_in), (vu_hbm, vu),
        (par_hbm, par_ref), (node_hbm, node_ref), (len_hbm, len_ref),
    )
    loads = [
        pltpu.make_async_copy(src, dst, in_sem.at[i])
        for i, (src, dst) in enumerate(pairs)
    ]
    for load in loads:
        load.start()

    barrier = pltpu.get_barrier_semaphore()
    peers = [sibling] + [at(0, 0, k) for k in range(1, 8)]
    peers += [at(k, 0, 0) for k in (1, 2, 3)] + [at(0, k, 0) for k in (1, 2, 3)]
    for peer in peers:
        pl.semaphore_signal(barrier, inc=1, device_id=peer, device_id_type=MESH)
    loads[0].wait()
    keys[z, c, x_hi] = lat_ref[...].reshape(4, 16, 512)
    pl.semaphore_wait(barrier, len(peers))

    sent = []

    def send(block, recv_sem, peer):
        copy = pltpu.make_async_remote_copy(
            src_ref=block, dst_ref=block, send_sem=ag_send.at[len(sent)], recv_sem=recv_sem,
            device_id=peer, device_id_type=MESH,
        )
        copy.start()
        sent.append(copy)

    def arrived(block, recv_sem):
        pltpu.make_async_remote_copy(
            src_ref=block, dst_ref=block, send_sem=ag_send.at[0], recv_sem=recv_sem,
            device_id=sibling, device_id_type=MESH,
        ).wait_recv()

    colour = lambda x, y: lax.rem(y + 2 * lax.rem(x, 2), 4)
    flip = device(x + 1 - 2 * lax.rem(x, 2), y, z, c)
    neighbours = (at(0, 1, 0), at(0, -1, 0), flip)
    mine = colour(x, y)
    theirs = (lax.rem(mine + 3, 4), lax.rem(mine + 1, 4), lax.rem(mine + 2, 4))
    kinds = (x_hi, 1 - x_hi)
    far_first = (4, 3, 5, 2, 6, 1, 7)
    near_first = (1, 7, 2, 6, 3, 5, 4)

    def spread_z(kind):
        for k in far_first:
            send(keys.at[z, c, kinds[kind], mine], z_recv.at[k - 1, kind], at(0, 0, k))

    send(keys.at[z, c, x_hi], x_recv.at[0], partner)
    spread_z(0)
    send(keys.at[z, c, x_hi], c_recv.at[7, 0], sibling)

    def latents_of(src_ref, mat, out_ref, out_t_ref, turned):
        wide[...] = src_ref[...].astype(F32).reshape(wide.shape)
        for h in range(8):
            rows = wide[pl.ds(h, 128, stride=8), :].astype(BF16)
            if turned:
                val = lax.dot_general(
                    rows, mat[h], (((1,), (1,)), ((), ())), preferred_element_type=F32
                )
            else:
                val = dot(rows, mat[h])
            low = val.astype(BF16)
            out_ref[h * 128 : (h + 1) * 128, :] = low
            out_t_ref[:, h * 128 : (h + 1) * 128] = low.T

    loads[1].wait()
    loads[2].wait()
    latents_of(q_in, ku, ql, ql_t, False)

    arrived(keys.at[z, c, 1 - x_hi], x_recv.at[0])
    spread_z(1)
    send(keys.at[z, c, 1 - x_hi], c_recv.at[7, 1], sibling)

    loads[3].wait()
    loads[4].wait()
    latents_of(g_in, vu, gl, gl_t, True)

    def spread_replicas(kind):
        for k in near_first:
            piece = keys.at[lax.rem(z - k + 8, 8), c, kinds[kind], mine]
            arrived(piece, z_recv.at[k - 1, kind])
            for i in range(3):
                send(piece, n_recv.at[k - 1, kind, i], neighbours[i])

    for load in loads[5:]:
        load.wait()
    above = lax.broadcasted_iota(jnp.int32, (256, 256), 0)
    below = lax.broadcasted_iota(jnp.int32, (256, 256), 1)
    linked = (above == par_ref[...]) | (above == below)
    reach = jnp.where(linked, 1.0, 0.0).astype(BF16)
    for _ in range(8):
        reach = jnp.minimum(dot(reach, reach), 1.0).astype(BF16)
    spot = lax.broadcasted_iota(jnp.int32, (256, 128), 1)
    node = lax.broadcasted_iota(jnp.int32, (256, 128), 0)
    token_node = jnp.full((256, 128), node_ref[0, 0], jnp.int32)
    bound = len_ref[0, 0]
    for b in range(1, 8):
        token_node = jnp.where(spot >= bound, node_ref[0, b], token_node)
        bound = bound + len_ref[0, b]
    picked = jnp.where(token_node == node, 1.0, 0.0).astype(BF16)
    live_t[...] = dot(reach, picked).astype(BF16)

    m_run[...] = jnp.full(m_run.shape, MASKED, F32)
    l_run[...] = jnp.zeros(l_run.shape, F32)
    d_run[...] = jnp.zeros(d_run.shape, F32)

    spread_replicas(0)

    def score_blocks(kind, planes):
        which = kinds[kind]
        rows = 128 * len(planes)
        row = lax.broadcasted_iota(jnp.int32, (rows, 256), 0)
        col = lax.broadcasted_iota(jnp.int32, (rows, 256), 1)
        plane_of = jnp.zeros((rows, 256), jnp.int32)
        for n, plane in enumerate(planes):
            plane_of = jnp.where(row // 128 == n, plane, plane_of)
        half, inner = lax.rem(row // 64, 2), lax.rem(row, 64) // NODE_LEN
        key_node = ((which * 8 + plane_of) * 2 + half) * NODE_LEN + inner
        spread = jnp.where(key_node == col, 1.0, 0.0).astype(BF16)
        bias = (dot(spread, live_t[...]) - 1.0) * (-MASKED)
        bias = jnp.concatenate([bias, bias], axis=1)
        group = jnp.concatenate([keys[plane, :, which].reshape(128, 512) for plane in planes], axis=0)
        for tile in range(4):
            cols = slice(tile * 256, (tile + 1) * 256)
            s = dot(group, ql_t[:, cols]) * (SCALE * LOG2E) + bias
            gw = dot(group, gl_t[:, cols])
            m_old = m_run[:, cols]
            m_new = jnp.maximum(m_old, jnp.max(s, axis=0, keepdims=True))
            w = jnp.exp2(s - m_new)
            alpha = jnp.exp2(m_old - m_new)
            l_run[:, cols] = alpha * l_run[:, cols] + jnp.sum(w, axis=0, keepdims=True)
            low = w.astype(BF16).astype(F32)
            d_run[:, cols] = alpha * d_run[:, cols] + jnp.sum(low * gw, axis=0, keepdims=True)
            m_run[:, cols] = m_new
            for n, plane in enumerate(planes):
                part = slice(n * 128, (n + 1) * 128)
                m_grp[plane, which, :, cols] = m_new
                w_buf[plane, :, which, :, cols] = w[part].reshape(2, 64, 256)
                gw_buf[plane, :, which, :, cols] = gw[part].reshape(2, 64, 256)

    def complete(kind, steps):
        for k in steps:
            block = keys.at[lax.rem(z - k + 8, 8), c, kinds[kind]]
            for i in range(3):
                piece = keys.at[lax.rem(z - k + 8, 8), c, kinds[kind], theirs[i]]
                arrived(piece, n_recv.at[k - 1, kind, i])
            send(block, c_recv.at[k - 1, kind], sibling)

    def score_from(kind, steps):
        planes = []
        for k in steps:
            plane = lax.rem(z - k + 8, 8)
            arrived(keys.at[plane, 1 - c, kinds[kind]], c_recv.at[(k - 1) % 8, kind])
            if kind == 1:
                keys_t[:, pl.ds(pl.multiple_of(plane * 256, 256), 256)] = (
                    keys[plane].reshape(256, 512).T
                )
            planes.append(plane)
        score_blocks(kind, planes)

    score_from(0, (0,))
    score_from(1, (0,))
    spread_replicas(1)
    complete(0, near_first)
    score_from(0, near_first[:4])
    complete(1, near_first[:4])
    score_from(0, near_first[4:])
    complete(1, near_first[4:])
    score_from(1, near_first[:4])
    score_from(1, near_first[4:])

    inv = 1.0 / l_run[...]
    l_run[...] = inv
    d_run[...] = d_run[...] * inv

    def core_copy(s):
        return pltpu.make_async_remote_copy(
            src_ref=core_out.at[s], dst_ref=core_in.at[s], send_sem=core_send.at[s],
            recv_sem=core_recv.at[s], device_id=sibling, device_id_type=MESH,
        )

    def axis_copies(s):
        copies = []
        for part in (0, 1):
            for k in (1, 2, 3):
                place_of = lax.rem((x if part == 0 else y) + k, 4)
                copies.append(
                    pltpu.make_async_remote_copy(
                        src_ref=axis_out.at[s, part, place_of], dst_ref=axis_in.at[s, part, k - 1],
                        send_sem=ax_send.at[s, part, k - 1], recv_sem=ax_recv.at[s, part, k - 1],
                        device_id=at(k, 0, 0) if part == 0 else at(0, k, 0), device_id_type=MESH,
                    )
                )
        return copies

    def z_copy(s):
        return pltpu.make_async_remote_copy(
            src_ref=z_out.at[s], dst_ref=z_in.at[s], send_sem=zs_send.at[s],
            recv_sem=zs_recv.at[s], device_id=at(0, 0, step_offset(s)), device_id_type=MESH,
        )

    def contribution(*steps):
        planes = [lax.rem(z + step_offset(s), 8) for s in steps]
        total = None
        for tile in range(4):
            cols = slice(tile * 256, (tile + 1) * 256)
            probs, grads = [], []
            for plane in planes:
                factor = [
                    jnp.exp2(m_grp[plane, which, :, cols] - m_run[:, cols]) * l_run[:, cols]
                    for which in (0, 1)
                ]
                for half in (0, 1):
                    for which in (0, 1):
                        p = w_buf[plane, half, which, :, cols] * factor[which]
                        gw = gw_buf[plane, half, which, :, cols]
                        grads.append((p * (gw - d_run[:, cols])).astype(BF16))
                        probs.append(p.astype(BF16))
                gs_buf[pl.ds(pl.multiple_of(plane * 256, 256), 256), cols] = jnp.concatenate(
                    grads[-4:], axis=0
                )
            gs, p_low = jnp.concatenate(grads, axis=0), jnp.concatenate(probs, axis=0)
            term = dot(gs, ql[cols, :]) * SCALE + dot(p_low, gl[cols, :])
            total = term if total is None else total + term
        for n, s in enumerate(steps):
            slot = s % 4
            cont[slot] = total[n * 256 : (n + 1) * 256].reshape(2, 2, 64, 512)
            for part in (0, 1):
                for j in range(4):
                    core_out[s, part, j] = cont[
                        slot, 1 - c, :, part * 32 : (part + 1) * 32, j * 128 : (j + 1) * 128
                    ].astype(BF16)
            core_copy(s).start()

    def core_sum(s):
        core_copy(s).wait()
        slot = s % 4
        for part in (0, 1):
            for j in range(4):
                axis_out[s, part, j] = (
                    cont[slot, c, :, part * 32 : (part + 1) * 32, j * 128 : (j + 1) * 128]
                    + core_in[s, part, j].astype(F32)
                ).astype(BF16)
        for copy in axis_copies(s):
            copy.start()

    def axis_sum(s, last):
        for copy in axis_copies(s):
            copy.wait()
        for part in (0, 1):
            total = axis_out[s, part, x if part == 0 else y].astype(F32)
            for k in range(3):
                total = total + axis_in[s, part, k].astype(F32)
            if last:
                z_own[part] = total
            else:
                z_out[s, part] = total.astype(BF16)
        if not last:
            z_copy(s).start()

    def query_tile(tile):
        cols = slice(tile * 512, (tile + 1) * 512)
        grad = (dot(keys_t[...], gs_buf[:, cols]) * SCALE).astype(BF16)
        for i in range(4):
            h = 4 * tile + i
            out = dot(ku[h], grad[:, i * 128 : (i + 1) * 128])
            wide[pl.ds(h, 128, stride=8), :] = out.T

    contribution(0)
    contribution(1, 2)
    core_sum(0)
    contribution(3, 4)
    core_sum(1)
    core_sum(2)
    axis_sum(0, False)
    contribution(5, 6)
    core_sum(3)
    core_sum(4)
    contribution(7)
    core_sum(5)
    core_sum(6)
    axis_sum(1, False)
    axis_sum(2, False)
    core_sum(7)
    axis_sum(3, False)
    axis_sum(4, False)
    query_tile(0)
    axis_sum(5, False)
    axis_sum(6, False)
    axis_sum(7, True)
    for s in range(7):
        z_copy(s).wait()
    for part in (0, 1):
        total = z_own[part]
        for s in range(7):
            total = total + z_in[s, part].astype(F32)
        if part == 0:
            sum_a[y] = total.astype(BF16)
        else:
            out_b[...] = total.astype(BF16)
            sum_b[x] = out_b[x_hi]

    first = []
    for k in (1, 2, 3):
        first.append(
            pltpu.make_async_remote_copy(
                src_ref=sum_a.at[y], dst_ref=sum_a.at[y], send_sem=t1_send.at[0, k - 1],
                recv_sem=t1_recv.at[0, k - 1], device_id=at(0, k, 0), device_id_type=MESH,
            )
        )
        their_hi = lax.rem(x + k, 4) // 2
        first.append(
            pltpu.make_async_remote_copy(
                src_ref=out_b.at[their_hi], dst_ref=sum_b.at[x], send_sem=t1_send.at[1, k - 1],
                recv_sem=t1_recv.at[1, k - 1], device_id=at(k, 0, 0), device_id_type=MESH,
            )
        )
    for copy in first:
        copy.start()
    query_tile(1)
    dq_ref[...] = wide[...].reshape(128, 8, 128).astype(BF16)
    for copy in first:
        copy.wait()

    out_a[...] = (
        sum_a[0].astype(F32) + sum_a[1].astype(F32) + sum_a[2].astype(F32) + sum_a[3].astype(F32)
    ).astype(BF16)
    last_a[x] = out_a[x_hi]
    last_b[y] = (
        sum_b[0].astype(F32) + sum_b[1].astype(F32) + sum_b[2].astype(F32) + sum_b[3].astype(F32)
    ).astype(BF16)
    second = []
    for k in (1, 2, 3):
        their_hi = lax.rem(x + k, 4) // 2
        second.append(
            pltpu.make_async_remote_copy(
                src_ref=out_a.at[their_hi], dst_ref=last_a.at[x], send_sem=t2_send.at[0, k - 1],
                recv_sem=t2_recv.at[0, k - 1], device_id=at(k, 0, 0), device_id_type=MESH,
            )
        )
        second.append(
            pltpu.make_async_remote_copy(
                src_ref=last_b.at[y], dst_ref=last_b.at[y], send_sem=t2_send.at[1, k - 1],
                recv_sem=t2_recv.at[1, k - 1], device_id=at(0, k, 0), device_id_type=MESH,
            )
        )
    for copy in second:
        copy.start()
    for copy in sent:
        copy.wait_send()
    for copy in second:
        copy.wait()
    for j in range(4):
        dl_ref[0:32, j * 128 : (j + 1) * 128] = last_a[j].astype(F32)
        dl_ref[32:64, j * 128 : (j + 1) * 128] = last_b[j].astype(F32)


def hand_over(dq_in, dl_in, dq_out, dl_out):
    dq_out[...] = dq_in[...]
    dl_out[...] = dl_in[...]


def on_device(
    latents, queries, grad_out, key_up_matrix, value_up_matrix, parents, branch_node, branch_lengths
):
    vmem = pl.BlockSpec(memory_space=pltpu.VMEM)
    dma = pltpu.SemaphoreType.DMA
    tile = (2, 32, 128)
    d_queries, d_latents = pl.pallas_call(
        kernel,
        name="tree_attention_backward",
        out_shape=(
            jax.ShapeDtypeStruct((128, 8, 128), BF16),
            jax.ShapeDtypeStruct((64, 512), F32),
        ),
        in_specs=[pl.BlockSpec(memory_space=pltpu.HBM)] * 8,
        out_specs=(vmem, vmem),
        scratch_shapes=[
            pltpu.VMEM((64, 512), BF16),
            pltpu.VMEM((1, 256), jnp.int32),
            pltpu.SMEM((1, 8), jnp.int32),
            pltpu.SMEM((1, 8), jnp.int32),
            pltpu.VMEM((128, 8, 128), BF16),
            pltpu.VMEM((128, 8, 128), BF16),
            pltpu.VMEM((8, 128, 512), BF16),
            pltpu.VMEM((8, 512, 128), BF16),
            pltpu.VMEM((1024, 128), F32),
            pltpu.VMEM((8, 2, 2, 4, 16, 512), BF16),
            pltpu.VMEM((512, 2048), BF16),
            pltpu.VMEM((1024, 512), BF16),
            pltpu.VMEM((1024, 512), BF16),
            pltpu.VMEM((512, 1024), BF16),
            pltpu.VMEM((512, 1024), BF16),
            pltpu.VMEM((256, 128), BF16),
            pltpu.VMEM((8, 2, 2, 64, 1024), F32),
            pltpu.VMEM((8, 2, 2, 64, 1024), F32),
            pltpu.VMEM((2048, 1024), BF16),
            pltpu.VMEM((8, 2, 1, 1024), F32),
            pltpu.VMEM((1, 1024), F32),
            pltpu.VMEM((1, 1024), F32),
            pltpu.VMEM((1, 1024), F32),
            pltpu.VMEM((4, 2, 2, 64, 512), F32),
            pltpu.VMEM((8, 2, 4) + tile, BF16),
            pltpu.VMEM((8, 2, 4) + tile, BF16),
            pltpu.VMEM((8, 2, 4) + tile, BF16),
            pltpu.VMEM((8, 2, 3) + tile, BF16),
            pltpu.VMEM((7, 2) + tile, BF16),
            pltpu.VMEM((7, 2) + tile, BF16),
            pltpu.VMEM((2,) + tile, F32),
            pltpu.VMEM((4,) + tile, BF16),
            pltpu.VMEM((4, 32, 128), BF16),
            pltpu.VMEM((4, 32, 128), BF16),
            pltpu.VMEM((4, 32, 128), BF16),
            pltpu.VMEM(tile, BF16),
            pltpu.VMEM(tile, BF16),
            dma((8,)),
            dma((73,)),
            dma((1,)),
            dma((7, 2)),
            dma((7, 2, 3)),
            dma((8, 2)),
            dma((8,)),
            dma((8,)),
            dma((8, 2, 3)),
            dma((8, 2, 3)),
            dma((7,)),
            dma((7,)),
            dma((2, 3)),
            dma((2, 3)),
            dma((2, 3)),
            dma((2, 3)),
        ],
        compiler_params=pltpu.CompilerParams(
            collective_id=0, has_side_effects=True, vmem_limit_bytes=58 * 1024 * 1024
        ),
    )(
        latents, parents.reshape(1, 256), branch_node, branch_lengths,
        queries, grad_out, key_up_matrix, value_up_matrix,
    )
    return pl.pallas_call(
        hand_over,
        name="hand_over",
        out_shape=(
            jax.ShapeDtypeStruct((128, 8, 128), BF16),
            jax.ShapeDtypeStruct((64, 512), F32),
        ),
        in_specs=[vmem, vmem],
        out_specs=(vmem, vmem),
    )(d_queries, d_latents)


def solution(mesh):
    placed = (
        P("leaf", None),
        P("leaf", "head", None),
        P("leaf", "head", None),
        P("head", None, None),
        P("head", None, None),
        P(),
        P("leaf", None),
        P("leaf", None),
    )
    return jax.shard_map(
        on_device,
        mesh=mesh,
        in_specs=placed,
        out_specs=(P("leaf", "head", None), P("leaf", None)),
        check_vma=False,
    )
```

```python
import jax
import jax.numpy as jnp
from jax import lax
from jax.experimental import pallas as pl
from jax.experimental.pallas import tpu as pltpu
from jax.sharding import PartitionSpec as P

MESH = pl.DeviceIdType.MESH
NODE_LEN = 8
SCALE = 192.0 ** (-0.5)
LOG2E = 1.4426950408889634
MASKED = -1e30
F32 = jnp.float32
BF16 = jnp.bfloat16


def dot(a, b):
    return jnp.dot(a, b, preferred_element_type=F32)


def place():
    leaf = lax.axis_index("leaf")
    head = lax.axis_index("head")
    x = (leaf // 16) * 2 + head // 4
    return x, lax.rem(head, 4), lax.rem(leaf // 2, 8), lax.rem(leaf, 2)


def device(x, y, z, c):
    return ((x // 2) * 16 + z * 2 + c, lax.rem(x, 2) * 4 + y)


def step_offset(s):
    return (4, 3, 5, 2, 6, 1, 7, 0)[s]


def kernel(
    lat_hbm, par_hbm, node_hbm, len_hbm, q_hbm, g_hbm, ku_hbm, vu_hbm,
    dq_ref, dl_ref,
    lat_ref, par_ref, node_ref, len_ref, q_in, g_in, ku, vu, wide, keys, keys_t, ql, gl, ql_t, gl_t, live_t,
    w_buf, gw_buf, gs_buf, m_grp, m_run, l_run, d_run,
    cont, core_out, core_in, axis_out, axis_in, z_out, z_in, z_own,
    sum_a, sum_b, last_a, last_b, out_a, out_b,
    in_sem, ag_send, x_recv, z_recv, n_recv, c_recv,
    core_send, core_recv, ax_send, ax_recv, zs_send, zs_recv,
    t1_send, t1_recv, t2_send, t2_recv,
):
    x, y, z, c = place()
    x_hi = x // 2
    at = lambda dx, dy, dz: device(
        lax.rem(x + dx + 4, 4), lax.rem(y + dy + 4, 4), lax.rem(z + dz + 8, 8), c
    )
    sibling = device(x, y, z, 1 - c)
    partner = device(3 - x, y, z, c)

    barrier = pltpu.get_barrier_semaphore()
    peers = [sibling] + [at(0, 0, k) for k in range(1, 8)]
    peers += [at(k, 0, 0) for k in (1, 2, 3)] + [at(0, k, 0) for k in (1, 2, 3)]
    for peer in peers:
        pl.semaphore_signal(barrier, inc=1, device_id=peer, device_id_type=MESH)
    pairs = (
        (lat_hbm, lat_ref), (q_hbm, q_in), (ku_hbm, ku), (g_hbm, g_in), (vu_hbm, vu),
        (par_hbm, par_ref), (node_hbm, node_ref), (len_hbm, len_ref),
    )
    loads = [
        pltpu.make_async_copy(src, dst, in_sem.at[i])
        for i, (src, dst) in enumerate(pairs)
    ]
    for load in loads:
        load.start()
    loads[0].wait()
    keys[z, c, x_hi] = lat_ref[...].reshape(4, 16, 512)
    pl.semaphore_wait(barrier, len(peers))

    sent = []

    def send(block, recv_sem, peer):
        copy = pltpu.make_async_remote_copy(
            src_ref=block, dst_ref=block, send_sem=ag_send.at[len(sent)], recv_sem=recv_sem,
            device_id=peer, device_id_type=MESH,
        )
        copy.start()
        sent.append(copy)

    def arrived(block, recv_sem):
        pltpu.make_async_remote_copy(
            src_ref=block, dst_ref=block, send_sem=ag_send.at[0], recv_sem=recv_sem,
            device_id=sibling, device_id_type=MESH,
        ).wait_recv()

    colour = lambda x, y: lax.rem(y + 2 * lax.rem(x, 2), 4)
    flip = device(x + 1 - 2 * lax.rem(x, 2), y, z, c)
    neighbours = (at(0, 1, 0), at(0, -1, 0), flip)
    mine = colour(x, y)
    theirs = (lax.rem(mine + 3, 4), lax.rem(mine + 1, 4), lax.rem(mine + 2, 4))
    kinds = (x_hi, 1 - x_hi)
    far_first = (4, 3, 5, 2, 6, 1, 7)
    near_first = (1, 7, 2, 6, 3, 5, 4)

    def spread_z(kind):
        for k in far_first:
            send(keys.at[z, c, kinds[kind], mine], z_recv.at[k - 1, kind], at(0, 0, k))

    send(keys.at[z, c, x_hi], x_recv.at[0], partner)
    spread_z(0)
    send(keys.at[z, c, x_hi], c_recv.at[7, 0], sibling)

    def latents_of(src_ref, mat, out_ref, out_t_ref, turned):
        wide[...] = src_ref[...].astype(F32).reshape(wide.shape)
        for h in range(8):
            rows = wide[pl.ds(h, 128, stride=8), :].astype(BF16)
            if turned:
                val = lax.dot_general(
                    rows, mat[h], (((1,), (1,)), ((), ())), preferred_element_type=F32
                )
            else:
                val = dot(rows, mat[h])
            low = val.astype(BF16)
            out_ref[h * 128 : (h + 1) * 128, :] = low
            out_t_ref[:, h * 128 : (h + 1) * 128] = low.T

    loads[1].wait()
    loads[2].wait()
    latents_of(q_in, ku, ql, ql_t, False)

    arrived(keys.at[z, c, 1 - x_hi], x_recv.at[0])
    spread_z(1)
    send(keys.at[z, c, 1 - x_hi], c_recv.at[7, 1], sibling)

    loads[3].wait()
    loads[4].wait()
    latents_of(g_in, vu, gl, gl_t, True)

    def spread_replicas(kind):
        for k in near_first:
            piece = keys.at[lax.rem(z - k + 8, 8), c, kinds[kind], mine]
            arrived(piece, z_recv.at[k - 1, kind])
            for i in range(3):
                send(piece, n_recv.at[k - 1, kind, i], neighbours[i])

    for load in loads[5:]:
        load.wait()
    above = lax.broadcasted_iota(jnp.int32, (256, 256), 0)
    below = lax.broadcasted_iota(jnp.int32, (256, 256), 1)
    linked = (above == par_ref[...]) | (above == below)
    reach = jnp.where(linked, 1.0, 0.0).astype(BF16)
    for _ in range(8):
        reach = jnp.minimum(dot(reach, reach), 1.0).astype(BF16)
    spot = lax.broadcasted_iota(jnp.int32, (256, 128), 1)
    node = lax.broadcasted_iota(jnp.int32, (256, 128), 0)
    token_node = jnp.full((256, 128), node_ref[0, 0], jnp.int32)
    bound = len_ref[0, 0]
    for b in range(1, 8):
        token_node = jnp.where(spot >= bound, node_ref[0, b], token_node)
        bound = bound + len_ref[0, b]
    picked = jnp.where(token_node == node, 1.0, 0.0).astype(BF16)
    live_t[...] = dot(reach, picked).astype(BF16)

    m_run[...] = jnp.full(m_run.shape, MASKED, F32)
    l_run[...] = jnp.zeros(l_run.shape, F32)
    d_run[...] = jnp.zeros(d_run.shape, F32)

    spread_replicas(0)

    def score_blocks(kind, planes):
        which = kinds[kind]
        rows = 128 * len(planes)
        row = lax.broadcasted_iota(jnp.int32, (rows, 256), 0)
        col = lax.broadcasted_iota(jnp.int32, (rows, 256), 1)
        plane_of = jnp.zeros((rows, 256), jnp.int32)
        for n, plane in enumerate(planes):
            plane_of = jnp.where(row // 128 == n, plane, plane_of)
        half, inner = lax.rem(row // 64, 2), lax.rem(row, 64) // NODE_LEN
        key_node = ((which * 8 + plane_of) * 2 + half) * NODE_LEN + inner
        spread = jnp.where(key_node == col, 1.0, 0.0).astype(BF16)
        bias = (dot(spread, live_t[...]) - 1.0) * (-MASKED)
        bias = jnp.concatenate([bias, bias], axis=1)
        group = jnp.concatenate([keys[plane, :, which].reshape(128, 512) for plane in planes], axis=0)
        for tile in range(4):
            cols = slice(tile * 256, (tile + 1) * 256)
            s = dot(group, ql_t[:, cols]) * (SCALE * LOG2E) + bias
            gw = dot(group, gl_t[:, cols])
            m_old = m_run[:, cols]
            m_new = jnp.maximum(m_old, jnp.max(s, axis=0, keepdims=True))
            w = jnp.exp2(s - m_new)
            alpha = jnp.exp2(m_old - m_new)
            l_run[:, cols] = alpha * l_run[:, cols] + jnp.sum(w, axis=0, keepdims=True)
            low = w.astype(BF16).astype(F32)
            d_run[:, cols] = alpha * d_run[:, cols] + jnp.sum(low * gw, axis=0, keepdims=True)
            m_run[:, cols] = m_new
            for n, plane in enumerate(planes):
                part = slice(n * 128, (n + 1) * 128)
                m_grp[plane, which, :, cols] = m_new
                w_buf[plane, :, which, :, cols] = w[part].reshape(2, 64, 256)
                gw_buf[plane, :, which, :, cols] = gw[part].reshape(2, 64, 256)

    def complete(kind, steps):
        for k in steps:
            block = keys.at[lax.rem(z - k + 8, 8), c, kinds[kind]]
            for i in range(3):
                piece = keys.at[lax.rem(z - k + 8, 8), c, kinds[kind], theirs[i]]
                arrived(piece, n_recv.at[k - 1, kind, i])
            send(block, c_recv.at[k - 1, kind], sibling)

    def score_from(kind, steps):
        planes = []
        for k in steps:
            plane = lax.rem(z - k + 8, 8)
            arrived(keys.at[plane, 1 - c, kinds[kind]], c_recv.at[(k - 1) % 8, kind])
            if kind == 1:
                keys_t[:, pl.ds(pl.multiple_of(plane * 256, 256), 256)] = (
                    keys[plane].reshape(256, 512).T
                )
            planes.append(plane)
        score_blocks(kind, planes)

    score_from(0, (0,))
    score_from(1, (0,))
    spread_replicas(1)
    complete(0, near_first)
    score_from(0, near_first[:4])
    complete(1, near_first[:4])
    score_from(0, near_first[4:])
    complete(1, near_first[4:])
    score_from(1, near_first[:4])
    score_from(1, near_first[4:])

    inv = 1.0 / l_run[...]
    l_run[...] = inv
    d_run[...] = d_run[...] * inv

    def core_copy(s):
        return pltpu.make_async_remote_copy(
            src_ref=core_out.at[s], dst_ref=core_in.at[s], send_sem=core_send.at[s],
            recv_sem=core_recv.at[s], device_id=sibling, device_id_type=MESH,
        )

    def axis_copies(s):
        copies = []
        for part in (0, 1):
            for k in (1, 2, 3):
                place_of = lax.rem((x if part == 0 else y) + k, 4)
                copies.append(
                    pltpu.make_async_remote_copy(
                        src_ref=axis_out.at[s, part, place_of], dst_ref=axis_in.at[s, part, k - 1],
                        send_sem=ax_send.at[s, part, k - 1], recv_sem=ax_recv.at[s, part, k - 1],
                        device_id=at(k, 0, 0) if part == 0 else at(0, k, 0), device_id_type=MESH,
                    )
                )
        return copies

    def z_copy(s):
        return pltpu.make_async_remote_copy(
            src_ref=z_out.at[s], dst_ref=z_in.at[s], send_sem=zs_send.at[s],
            recv_sem=zs_recv.at[s], device_id=at(0, 0, step_offset(s)), device_id_type=MESH,
        )

    def contribution(*steps):
        planes = [lax.rem(z + step_offset(s), 8) for s in steps]
        total = None
        for tile in range(4):
            cols = slice(tile * 256, (tile + 1) * 256)
            probs, grads = [], []
            for plane in planes:
                factor = [
                    jnp.exp2(m_grp[plane, which, :, cols] - m_run[:, cols]) * l_run[:, cols]
                    for which in (0, 1)
                ]
                for half in (0, 1):
                    for which in (0, 1):
                        p = w_buf[plane, half, which, :, cols] * factor[which]
                        gw = gw_buf[plane, half, which, :, cols]
                        grads.append((p * (gw - d_run[:, cols])).astype(BF16))
                        probs.append(p.astype(BF16))
                gs_buf[pl.ds(pl.multiple_of(plane * 256, 256), 256), cols] = jnp.concatenate(
                    grads[-4:], axis=0
                )
            gs, p_low = jnp.concatenate(grads, axis=0), jnp.concatenate(probs, axis=0)
            term = dot(gs, ql[cols, :]) * SCALE + dot(p_low, gl[cols, :])
            total = term if total is None else total + term
        for n, s in enumerate(steps):
            slot = s % 4
            cont[slot] = total[n * 256 : (n + 1) * 256].reshape(2, 2, 64, 512)
            for part in (0, 1):
                for j in range(4):
                    core_out[s, part, j] = cont[
                        slot, 1 - c, :, part * 32 : (part + 1) * 32, j * 128 : (j + 1) * 128
                    ].astype(BF16)
            core_copy(s).start()

    def core_sum(s):
        core_copy(s).wait()
        slot = s % 4
        for part in (0, 1):
            for j in range(4):
                axis_out[s, part, j] = (
                    cont[slot, c, :, part * 32 : (part + 1) * 32, j * 128 : (j + 1) * 128]
                    + core_in[s, part, j].astype(F32)
                ).astype(BF16)
        for copy in axis_copies(s):
            copy.start()

    def axis_sum(s, last):
        for copy in axis_copies(s):
            copy.wait()
        for part in (0, 1):
            total = axis_out[s, part, x if part == 0 else y].astype(F32)
            for k in range(3):
                total = total + axis_in[s, part, k].astype(F32)
            if last:
                z_own[part] = total
            else:
                z_out[s, part] = total.astype(BF16)
        if not last:
            z_copy(s).start()

    def query_tile(tile):
        cols = slice(tile * 512, (tile + 1) * 512)
        grad = (dot(keys_t[...], gs_buf[:, cols]) * SCALE).astype(BF16)
        for i in range(4):
            h = 4 * tile + i
            out = dot(ku[h], grad[:, i * 128 : (i + 1) * 128])
            wide[pl.ds(h, 128, stride=8), :] = out.T

    contribution(0)
    contribution(1, 2)
    core_sum(0)
    contribution(3, 4)
    core_sum(1)
    core_sum(2)
    axis_sum(0, False)
    contribution(5, 6)
    core_sum(3)
    core_sum(4)
    contribution(7)
    core_sum(5)
    core_sum(6)
    axis_sum(1, False)
    axis_sum(2, False)
    core_sum(7)
    axis_sum(3, False)
    axis_sum(4, False)
    query_tile(0)
    axis_sum(5, False)
    axis_sum(6, False)
    axis_sum(7, True)
    for s in range(7):
        z_copy(s).wait()
    for part in (0, 1):
        total = z_own[part]
        for s in range(7):
            total = total + z_in[s, part].astype(F32)
        if part == 0:
            sum_a[y] = total.astype(BF16)
        else:
            out_b[...] = total.astype(BF16)
            sum_b[x] = out_b[x_hi]

    first = []
    for k in (1, 2, 3):
        first.append(
            pltpu.make_async_remote_copy(
                src_ref=sum_a.at[y], dst_ref=sum_a.at[y], send_sem=t1_send.at[0, k - 1],
                recv_sem=t1_recv.at[0, k - 1], device_id=at(0, k, 0), device_id_type=MESH,
            )
        )
        their_hi = lax.rem(x + k, 4) // 2
        first.append(
            pltpu.make_async_remote_copy(
                src_ref=out_b.at[their_hi], dst_ref=sum_b.at[x], send_sem=t1_send.at[1, k - 1],
                recv_sem=t1_recv.at[1, k - 1], device_id=at(k, 0, 0), device_id_type=MESH,
            )
        )
    for copy in first:
        copy.start()
    query_tile(1)
    dq_ref[...] = wide[...].reshape(128, 8, 128).astype(BF16)
    for copy in first:
        copy.wait()

    out_a[...] = (
        sum_a[0].astype(F32) + sum_a[1].astype(F32) + sum_a[2].astype(F32) + sum_a[3].astype(F32)
    ).astype(BF16)
    last_a[x] = out_a[x_hi]
    last_b[y] = (
        sum_b[0].astype(F32) + sum_b[1].astype(F32) + sum_b[2].astype(F32) + sum_b[3].astype(F32)
    ).astype(BF16)
    second = []
    for k in (1, 2, 3):
        their_hi = lax.rem(x + k, 4) // 2
        second.append(
            pltpu.make_async_remote_copy(
                src_ref=out_a.at[their_hi], dst_ref=last_a.at[x], send_sem=t2_send.at[0, k - 1],
                recv_sem=t2_recv.at[0, k - 1], device_id=at(k, 0, 0), device_id_type=MESH,
            )
        )
        second.append(
            pltpu.make_async_remote_copy(
                src_ref=last_b.at[y], dst_ref=last_b.at[y], send_sem=t2_send.at[1, k - 1],
                recv_sem=t2_recv.at[1, k - 1], device_id=at(0, k, 0), device_id_type=MESH,
            )
        )
    for copy in second:
        copy.start()
    for copy in sent:
        copy.wait_send()
    for copy in second:
        copy.wait()
    for j in range(4):
        dl_ref[0:32, j * 128 : (j + 1) * 128] = last_a[j].astype(F32)
        dl_ref[32:64, j * 128 : (j + 1) * 128] = last_b[j].astype(F32)


def hand_over(dq_in, dl_in, dq_out, dl_out):
    dq_out[...] = dq_in[...]
    dl_out[...] = dl_in[...]


def on_device(
    latents, queries, grad_out, key_up_matrix, value_up_matrix, parents, branch_node, branch_lengths
):
    vmem = pl.BlockSpec(memory_space=pltpu.VMEM)
    dma = pltpu.SemaphoreType.DMA
    tile = (2, 32, 128)
    d_queries, d_latents = pl.pallas_call(
        kernel,
        name="tree_attention_backward",
        out_shape=(
            jax.ShapeDtypeStruct((128, 8, 128), BF16),
            jax.ShapeDtypeStruct((64, 512), F32),
        ),
        in_specs=[pl.BlockSpec(memory_space=pltpu.HBM)] * 8,
        out_specs=(vmem, vmem),
        scratch_shapes=[
            pltpu.VMEM((64, 512), BF16),
            pltpu.VMEM((1, 256), jnp.int32),
            pltpu.SMEM((1, 8), jnp.int32),
            pltpu.SMEM((1, 8), jnp.int32),
            pltpu.VMEM((128, 8, 128), BF16),
            pltpu.VMEM((128, 8, 128), BF16),
            pltpu.VMEM((8, 128, 512), BF16),
            pltpu.VMEM((8, 512, 128), BF16),
            pltpu.VMEM((1024, 128), F32),
            pltpu.VMEM((8, 2, 2, 4, 16, 512), BF16),
            pltpu.VMEM((512, 2048), BF16),
            pltpu.VMEM((1024, 512), BF16),
            pltpu.VMEM((1024, 512), BF16),
            pltpu.VMEM((512, 1024), BF16),
            pltpu.VMEM((512, 1024), BF16),
            pltpu.VMEM((256, 128), BF16),
            pltpu.VMEM((8, 2, 2, 64, 1024), F32),
            pltpu.VMEM((8, 2, 2, 64, 1024), F32),
            pltpu.VMEM((2048, 1024), BF16),
            pltpu.VMEM((8, 2, 1, 1024), F32),
            pltpu.VMEM((1, 1024), F32),
            pltpu.VMEM((1, 1024), F32),
            pltpu.VMEM((1, 1024), F32),
            pltpu.VMEM((4, 2, 2, 64, 512), F32),
            pltpu.VMEM((8, 2, 4) + tile, BF16),
            pltpu.VMEM((8, 2, 4) + tile, BF16),
            pltpu.VMEM((8, 2, 4) + tile, BF16),
            pltpu.VMEM((8, 2, 3) + tile, BF16),
            pltpu.VMEM((7, 2) + tile, BF16),
            pltpu.VMEM((7, 2) + tile, BF16),
            pltpu.VMEM((2,) + tile, F32),
            pltpu.VMEM((4,) + tile, BF16),
            pltpu.VMEM((4, 32, 128), BF16),
            pltpu.VMEM((4, 32, 128), BF16),
            pltpu.VMEM((4, 32, 128), BF16),
            pltpu.VMEM(tile, BF16),
            pltpu.VMEM(tile, BF16),
            dma((8,)),
            dma((73,)),
            dma((1,)),
            dma((7, 2)),
            dma((7, 2, 3)),
            dma((8, 2)),
            dma((8,)),
            dma((8,)),
            dma((8, 2, 3)),
            dma((8, 2, 3)),
            dma((7,)),
            dma((7,)),
            dma((2, 3)),
            dma((2, 3)),
            dma((2, 3)),
            dma((2, 3)),
        ],
        compiler_params=pltpu.CompilerParams(
            collective_id=0, has_side_effects=True, vmem_limit_bytes=58 * 1024 * 1024
        ),
    )(
        latents, parents.reshape(1, 256), branch_node, branch_lengths,
        queries, grad_out, key_up_matrix, value_up_matrix,
    )
    return pl.pallas_call(
        hand_over,
        name="hand_over",
        out_shape=(
            jax.ShapeDtypeStruct((128, 8, 128), BF16),
            jax.ShapeDtypeStruct((64, 512), F32),
        ),
        in_specs=[vmem, vmem],
        out_specs=(vmem, vmem),
    )(d_queries, d_latents)


def solution(mesh):
    placed = (
        P("leaf", None),
        P("leaf", "head", None),
        P("leaf", "head", None),
        P("head", None, None),
        P("head", None, None),
        P(),
        P("leaf", None),
        P("leaf", None),
    )
    return jax.shard_map(
        on_device,
        mesh=mesh,
        in_specs=placed,
        out_specs=(P("leaf", "head", None), P("leaf", None)),
        check_vma=False,
    )
```
